32 devices in a mesh: box: 4 (over z), row: 4 (over y, core), col: 2 (over x).
Axes of the slice: x: 2, y: 2, z: 4, core: 2. Of those that a mesh axis runs over, the one named last changes fastest.
Arguments:
- ext_ext: float32 [4, 3072, 3072], P('box', 'row', 'col'), may hold values from -6 to 6
- ext_int: float32 [4, 3072, 1024], P('box', 'row', 'col'), may hold values from -0.1875 to 0.1875
- int_ext: float32 [4, 1024, 3072], P('box', 'row', 'col'), may hold values from -6 to 6
- int_int: float32 [4, 1024, 1024], P('box', 'row', 'col'), may hold values from -0.1 to 0.1, as said below
Outputs:
- merged: float32 [4, 3072, 2, 3072], P('box', 'row', None, 'col')
The draws below stay inside these ranges and needn't reach their ends.
Inputs may be any that keep to these rules, and one draw needn't show every extreme that they name: `int_int`: independent entries.
All inputs are finite; a program needn't handle non-finite values.
Results may differ from the reference program's by a relative error of at most 0.0003.
Values sent between devices are 32-bit elements; how exact they have to be, the bound alone decides.
No kernel may reach another device: no remote copies, remote signals or barrier semaphores. Data moves between devices by JAX's collectives and lax.ppermute only.
A program may use at most 128 MiB of HBM per device.

```python
import jax
import jax.numpy as jnp
from jax import lax

NE = 3072
NI = 1024
BOXES = 4


def draw_int_int(key, part):
    scale = 0.8 / NI ** 0.5
    values = jnp.clip(jax.random.normal(key, (BOXES, NI, NI), jnp.float32), -4.0, 4.0)
    return values * scale


def block_levels(stream_key, extent, split, smallest, largest):
    def one(dim, shards_of):
        draws = jax.random.uniform(jax.random.fold_in(jax.random.fold_in(stream_key, 6), dim), (shards_of,), jnp.float32, smallest / len(split), largest / len(split))
        return jnp.repeat(jnp.exp(draws), extent[dim] // shards_of).reshape((-1,) + (1,) * (len(extent) - dim - 1))

    loudness = one(*split[0])
    for cut in split[1:]:
        loudness = loudness * one(*cut)
    return loudness


def noise(stream_key, dims, spread, bound, pieces=(), held_as=jnp.bfloat16):
    drawn = jax.random.normal(stream_key, dims, jnp.float32) * spread
    if len(pieces) > 0:
        drawn = block_levels(stream_key, dims, pieces, -0.22, 0.18) * drawn
    return jnp.clip(drawn, min=-bound, max=bound).astype(held_as)


def setup_inputs(seed: int = 0) -> dict:
    key_list = jax.random.split(jax.random.key(seed), 5)
    ext_ext = noise(key_list[0], (BOXES, NE, NE), 1.0, 6.0, ((0, 4), (1, 4), (2, 2)), jnp.float32)
    ext_int = noise(key_list[1], (BOXES, NE, NI), NI ** -0.5, 0.1875, ((0, 4), (1, 4), (2, 2)), jnp.float32)
    int_ext = noise(key_list[2], (BOXES, NI, NE), 1.0, 6.0, ((0, 4), (1, 4), (2, 2)), jnp.float32)
    int_int = draw_int_int(jax.random.fold_in(key_list[4], 71), 0)
    return {"ext_ext": ext_ext, "ext_int": ext_int, "int_ext": int_ext, "int_int": int_int}


def merge_one(items):
    ee, ed, de, dd, partner_de, partner_dd, parity = items
    hi = lax.Precision.HIGHEST
    coupling = jnp.dot(partner_dd, dd, precision=hi, preferred_element_type=jnp.float32)
    square = jnp.dot(coupling, coupling, precision=hi, preferred_element_type=jnp.float32)
    first = jnp.eye(NI, dtype=coupling.dtype) + coupling
    inverse = first + jnp.dot(first, square, precision=hi, preferred_element_type=jnp.float32)
    coupled = jnp.dot(partner_dd, de, precision=hi, preferred_element_type=jnp.float32)
    is_even = parity == 0
    source_zero = jnp.where(is_even, coupled, partner_de)
    source_one = jnp.where(is_even, partner_de, coupled)
    carried_zero = jnp.dot(inverse, source_zero, precision=hi, preferred_element_type=jnp.float32)
    carried_one = jnp.dot(inverse, source_one, precision=hi, preferred_element_type=jnp.float32)
    zeros = jnp.zeros_like(ee)
    merged_zero = jnp.where(is_even, ee, zeros) + jnp.dot(ed, carried_zero, precision=hi, preferred_element_type=jnp.float32)
    merged_one = jnp.where(is_even, zeros, ee) + jnp.dot(ed, carried_one, precision=hi, preferred_element_type=jnp.float32)
    return jnp.stack([merged_zero, merged_one], axis=1)


def swapped(array):
    shape = array.shape
    return array.reshape((BOXES // 2, 2) + shape[1:])[:, ::-1].reshape(shape)


def reference(ext_ext, ext_int, int_ext, int_int):
    parity = (jnp.arange(BOXES) % 2).astype(jnp.int32)
    items = (ext_ext, ext_int, int_ext, int_int, swapped(int_ext), swapped(int_int), parity)
    return lax.map(merge_one, items)
```

```python
import functools

import jax
import jax.numpy as jnp
from jax import lax
from jax.experimental import pallas as pl
from jax.experimental.layout import Layout, with_layout_constraint
from jax.experimental.pallas import tpu as pltpu
from jax.sharding import PartitionSpec as P

LANES = 128
VMEM_LIMIT = 60 * 2**20
F32 = jnp.float32
BF16 = jnp.bfloat16


def flipped(block, axis, bit):
    return lax.ppermute(block, axis, [(i, i ^ bit) for i in range(lax.axis_size(axis))])


def widened(block, axis, bits, dim):
    for bit in bits:
        other = flipped(block, axis, bit)
        first = (lax.axis_index(axis) & bit) == 0
        block = jnp.concatenate(
            [jnp.where(first, block, other), jnp.where(first, other, block)], axis=dim
        )
    return block


def halves(value):
    high = value.astype(BF16)
    return high, (value - high.astype(F32)).astype(BF16)


def dot(left, right):
    return jnp.dot(left, right, preferred_element_type=F32)


def dot3(left_high, left_low, right_high, right_low):
    return dot(left_high, right_high) + (dot(left_high, right_low) + dot(left_low, right_high))


def params():
    return pltpu.CompilerParams(vmem_limit_bytes=VMEM_LIMIT)


def inverse_kernel(places, where_ref, *refs):
    count = len(places)
    blocks = refs[:count]
    inv_high, inv_low, dp_high, dp_low = refs[count : count + 4]
    db_high, db_low, c_high, c_low, s_high, s_low = refs[count + 4 :]
    row, col = where_ref[0], where_ref[1]
    for ref, (partner, row_flip, col_flip, start) in zip(blocks, places, strict=True):
        high, low = halves(ref[...])
        full = blocks[0].shape[0]
        at = (row ^ row_flip) * full + start
        side = col ^ col_flip
        rows = pl.ds(pl.multiple_of(at, 8), ref.shape[0])
        to_high, to_low = (dp_high, dp_low) if partner else (db_high, db_low)
        to_high[side, rows, :] = high
        to_low[side, rows, :] = low
    parts, points, width = db_high.shape
    tile = 256

    def product(lh, ll, rh, rl, store):
        def body(step, carry):
            rows = pl.ds(pl.multiple_of(step * tile, tile), tile)
            for n in range(parts):
                total = None
                for k in range(parts):
                    inner = pl.ds(k * width, width)
                    term = dot3(lh[k, rows, :], ll[k, rows, :], rh[n, inner, :], rl[n, inner, :])
                    total = term if total is None else total + term
                store(step, n, rows, total)
            return carry

        lax.fori_loop(0, points // tile, body, 0)

    def keep(to_high, to_low):
        def store(step, n, rows, value):
            to_high[n, rows, :], to_low[n, rows, :] = halves(value)

        return store

    def finish(step, n, rows, value):
        row_ids = step * tile + lax.broadcasted_iota(jnp.int32, (tile, width), 0)
        col_ids = n * width + lax.broadcasted_iota(jnp.int32, (tile, width), 1)
        value = value + (s_high[n, rows, :].astype(F32) + s_low[n, rows, :].astype(F32))
        value = value + (c_high[n, rows, :].astype(F32) + c_low[n, rows, :].astype(F32))
        value = value + (row_ids == col_ids).astype(F32)
        inv_high[n, rows, :], inv_low[n, rows, :] = halves(value)

    product(dp_high, dp_low, db_high, db_low, keep(c_high, c_low))
    product(c_high, c_low, c_high, c_low, keep(s_high, s_low))
    product(c_high, c_low, s_high, s_low, finish)


def truncated_inverse(where, blocks, places, points):
    width = blocks[0].shape[1]
    parts = points // width
    shape = (parts, points, width)
    whole = pl.BlockSpec(memory_space=pltpu.VMEM)
    flops = 2 * 9 * points**3
    moved = 4 * 2 * points**2 + 4 * 2 * points**2
    return pl.pallas_call(
        functools.partial(inverse_kernel, places),
        out_shape=[jax.ShapeDtypeStruct(shape, BF16)] * 4,
        in_specs=[pl.BlockSpec(memory_space=pltpu.SMEM)] + [whole] * len(blocks),
        out_specs=[whole] * 4,
        scratch_shapes=[pltpu.VMEM(shape, BF16)] * 6,
        compiler_params=params(),
        cost_estimate=pl.CostEstimate(flops=flops, bytes_accessed=moved, transcendentals=0),
        name="inverse",
    )(where, *blocks)


def left_kernel(where_ref, own_ref, other_ref, ih, il, ph, pw, wh, wl, vh, vl, eh, el):
    col = where_ref[1]
    eh[col], el[col] = halves(own_ref[...])
    eh[col ^ 1], el[col ^ 1] = halves(other_ref[...])
    parts, points, width = ih.shape
    blocks, rows, depth = wh.shape
    for n in range(blocks):
        part, lane = divmod(n * depth, width)
        total = None
        for k in range(parts):
            inner = pl.ds(k * width, width)
            lanes = pl.ds(lane, depth)
            term = dot3(eh[k], el[k], ih[part, inner, lanes], il[part, inner, lanes])
            total = term if total is None else total + term
        wh[n], wl[n] = halves(total)
    for n in range(blocks):
        part, lane = divmod(n * depth, width)
        total = None
        for k in range(blocks):
            inner = pl.ds(k * depth, depth)
            lanes = pl.ds(lane, depth)
            term = dot3(wh[k], wl[k], ph[part, inner, lanes], pw[part, inner, lanes])
            total = term if total is None else total + term
        vh[n], vl[n] = halves(total)


def left_factors(where, own, other, inv_high, inv_low, dp_high, dp_low, depth):
    rows = own.shape[0]
    parts, points, width = inv_high.shape
    whole = pl.BlockSpec(memory_space=pltpu.VMEM)
    shape = (points // depth, rows, depth)
    return pl.pallas_call(
        left_kernel,
        out_shape=[jax.ShapeDtypeStruct(shape, BF16)] * 4,
        in_specs=[pl.BlockSpec(memory_space=pltpu.SMEM)] + [whole] * 6,
        out_specs=[whole] * 4,
        scratch_shapes=[pltpu.VMEM((parts, rows, width), BF16)] * 2,
        compiler_params=params(),
        cost_estimate=pl.CostEstimate(
            flops=12 * rows * points**2,
            bytes_accessed=8 * points**2 + 12 * rows * points,
            transcendentals=0,
        ),
        name="left",
    )(where, own, other, inv_high, inv_low, dp_high, dp_low)


def accumulate(total, row, full, left_high, left_low, refs, places):
    groups = {}
    for ref, (flip, start) in zip(refs, places, strict=True):
        groups.setdefault(flip, []).append((start, ref))
    for flip, pieces in groups.items():
        pieces.sort(key=lambda piece: piece[0])
        panel = jnp.concatenate([ref[...] for _, ref in pieces], axis=0)
        high, low = halves(panel)
        index = row ^ flip
        term = dot3(left_high[index], left_low[index], high, low)
        total = term if total is None else total + term
    return total


def start_kernel(places, full, where_ref, left_high, left_low, ee_ref, *refs):
    panels, out_ref = refs[:-1], refs[-1]
    out_ref[...] = accumulate(ee_ref[...], where_ref[0], full, left_high, left_low, panels, places)


def finish_kernel(places, full, where_ref, left_high, left_low, done_ref, *refs):
    panels, out_ref = refs[:-1], refs[-1]
    value = accumulate(None, where_ref[0], full, left_high, left_low, panels, places)
    lanes = out_ref.shape[-1]
    rows, cols = done_ref.shape
    sublanes = 2 * cols // lanes
    flat = out_ref if len(out_ref.shape) == 2 else out_ref.reshape(rows * sublanes, lanes)
    slot = where_ref[2]
    for tile in range(sublanes // 2):
        cols = slice(tile * lanes, (tile + 1) * lanes)
        flat[pl.ds(2 * tile + slot, rows, stride=sublanes), :] = done_ref[:, cols]
        flat[pl.ds(2 * tile + 1 - slot, rows, stride=sublanes), :] = value[:, cols]


def tile_cols(cols):
    return 4 * LANES if cols % (4 * LANES) == 0 else cols


def right_product(kernel, where, left, extra, panels, places, full, interleave):
    blocks, rows, depth = left[0].shape
    cols = extra.shape[1]
    step = tile_cols(cols)
    fixed = pl.BlockSpec((blocks, rows, depth), lambda n: (0, 0, 0), pipeline_mode=pl.Buffered(1))
    if interleave:
        group = 2 * step // LANES
        if group % 8:
            out_shape = jax.ShapeDtypeStruct((rows * group, LANES), F32)
            out_spec = pl.BlockSpec((rows * group, LANES), lambda n: (0, 0))
        else:
            out_shape = jax.ShapeDtypeStruct((rows, 2 * cols // LANES, LANES), F32)
            out_spec = pl.BlockSpec((rows, group, LANES), lambda n: (0, n, 0))
    else:
        out_shape = jax.ShapeDtypeStruct((rows, cols), F32)
        out_spec = pl.BlockSpec((rows, step), lambda n: (0, n))
    return pl.pallas_call(
        functools.partial(kernel, places, full),
        out_shape=out_shape,
        grid=(cols // step,),
        in_specs=[pl.BlockSpec(memory_space=pltpu.SMEM), fixed, fixed]
        + [pl.BlockSpec((rows, step), lambda n: (0, n))]
        + [pl.BlockSpec((panel.shape[0], step), lambda n: (0, n)) for panel in panels],
        out_specs=out_spec,
        compiler_params=params(),
        cost_estimate=pl.CostEstimate(
            flops=6 * rows * blocks * depth * cols,
            bytes_accessed=4 * (rows * blocks * depth + 2 * rows * cols + blocks * depth * cols),
            transcendentals=0,
        ),
        name="finish" if interleave else "start",
    )(where, *left, extra, *panels)


def local(ext_ext, ext_int, int_ext, int_int):
    ee, ed, de, dd = ext_ext[0], ext_int[0], int_ext[0], int_int[0]
    row_count, col_count = lax.axis_size("row"), lax.axis_size("col")
    points = dd.shape[0] * row_count
    col_bits = [1 << b for b in range(col_count.bit_length() - 2)]
    row_bits = [1 << b for b in range(1, row_count.bit_length() - 2)]
    col_top, row_top = col_count >> 1, row_count >> 1
    dd = widened(widened(dd, "col", col_bits, 1), "row", row_bits, 0)
    ed = widened(ed, "col", col_bits, 1)
    de = widened(de, "row", row_bits, 0)
    col = lax.axis_index("col") // col_top
    high = lax.axis_index("row") // row_top
    core = lax.axis_index("row") % 2
    slot = lax.axis_index("box") % 2
    where = jnp.stack([high * 2 + core, col, slot]).astype(jnp.int32)

    def over_x(block):
        return flipped(block, "col", col_top)

    def over_y(block):
        return flipped(block, "row", row_top)

    def over_z(block):
        return flipped(block, "box", 1)

    def over_core(block):
        return flipped(block, "row", 1)

    half = dd.shape[0] // 2
    dx, dy, dz = over_x(dd), over_y(dd), over_z(dd)
    dxy, dyz, dxz = over_x(dy), over_y(dz), over_z(dx)
    far_top = over_y(dxz[:half])
    far_low = over_z(dxy[half:])
    ed_other = over_x(ed)
    blocks, places = [], []
    for block, partner, row_flip, col_flip, start in (
        (dd, 0, 0, 0, 0),
        (dx, 0, 0, 1, 0),
        (dy, 0, 2, 0, 0),
        (dxy, 0, 2, 1, 0),
        (dz, 1, 0, 0, 0),
        (dxz, 1, 0, 1, 0),
        (dyz, 1, 2, 0, 0),
        (far_top, 1, 2, 1, 0),
        (far_low, 1, 2, 1, half),
    ):
        blocks += [block, over_core(block)]
        places += [(partner, row_flip, col_flip, start), (partner, row_flip ^ 1, col_flip, start)]
    inv_high, inv_low, dp_high, dp_low = truncated_inverse(where, blocks, tuple(places), points)
    wh, wl, vh, vl = left_factors(
        where, ed, ed_other, inv_high, inv_low, dp_high, dp_low, de.shape[0]
    )

    full = de.shape[0]
    half = full // 2
    de_top, de_low = de[:half], de[half:]
    y_low = over_y(de_low)
    z_top = over_z(de_top)
    y_top = over_y(de_top)
    z_low = over_z(de_low)
    far_top = over_y(z_top)
    far_low = over_z(y_low)
    own, own_places = [de, over_core(de)], [(0, 0), (1, 0)]
    for block, start in ((y_top, 0), (y_low, half)):
        own += [block, over_core(block)]
        own_places += [(2, start), (3, start)]
    partner, partner_places = [], []
    for block, flip, start in (
        (z_top, 0, 0),
        (z_low, 0, half),
        (far_top, 2, 0),
        (far_low, 2, half),
    ):
        partner += [block, over_core(block)]
        partner_places += [(flip, start), (flip ^ 1, start)]
    done = right_product(start_kernel, where, (vh, vl), ee, own, own_places, full, False)
    out = right_product(finish_kernel, where, (wh, wl), done, partner, partner_places, full, True)
    rows, cols = ee.shape
    out = out.reshape(rows, cols // LANES, 2, LANES).transpose(0, 2, 1, 3)
    out = with_layout_constraint(out, Layout(major_to_minor=(0, 2, 1, 3)))
    return out.reshape(1, rows, 2, cols)


def solution(mesh):
    placed = P("box", "row", "col")
    return jax.shard_map(
        local,
        mesh=mesh,
        in_specs=(placed,) * 4,
        out_specs=P("box", "row", None, "col"),
        check_vma=False,
    )
```
